256 devices in a mesh: layer: 16 (over y_lo, z), latent: 16 (over y_hi, x, core).
Axes of the slice: x: 4, y: 4 (y_hi: 2, y_lo: 2; y = y_hi * 2 + y_lo), z: 8, core: 2. Of those that a mesh axis runs over, the one named last changes fastest.
Arguments:
- layer_inputs: bfloat16 [384, 16384], P('latent', 'layer'), may hold values from -6 to 6
- mlp_outputs: bfloat16 [384, 16384], P('latent', 'layer'), may hold values from -6 to 6
- enc_weight: bfloat16 [16384, 4096], P('layer', 'latent'), may hold values from -0.125 to 0.125
- enc_bias: float32 [8, 4096], P(None, 'latent'), may hold values from -1 to 0.5
- dec_weight: bfloat16 [8, 4096, 16384], P(None, 'latent', 'layer'), may hold values from -0.03125 to 0.03125
Outputs:
- enc_grad: float32 [16384, 4096], P('layer', 'latent')
- dec_grad: bfloat16 [8, 4096, 16384], P(None, 'latent', 'layer')
The draws below stay inside these ranges and needn't reach their ends.
All inputs are finite; a program needn't handle non-finite values.
Results may differ from the reference program's by a relative error of at most 0.011.
Values may be sent and summed in bfloat16 or wider, within the bound.
No kernel may reach another device: no remote copies, remote signals or barrier semaphores. Data moves between devices by JAX's collectives and lax.ppermute only.
A program may use at most 64 MiB of HBM per device.

```python
import jax
import jax.numpy as jnp
from jax import lax

D = 2048
F = 4096
ROWS = 384
LAYERS = 8


def level_of(rng, extent, pieces, low, largest):
    def one(dim, blocks):
        steps = jax.random.uniform(jax.random.fold_in(jax.random.fold_in(rng, 6), dim), (blocks,), jnp.float32, low / len(pieces), largest / len(pieces))
        return jnp.repeat(jnp.exp(steps), extent[dim] // blocks).reshape((-1,) + (1,) * (len(extent) - dim - 1))

    loudness = one(*pieces[0])
    for cut in pieces[1:]:
        loudness = loudness * one(*cut)
    return loudness


def gaussian(rng, extent, deviation, most, pieces=(), held_as=jnp.bfloat16):
    gain = level_of(rng, extent, pieces, -0.22, 0.18) if pieces else 1.0
    values = jax.random.normal(rng, extent, jnp.float32) * deviation * gain
    return jnp.minimum(jnp.maximum(values, -most), most).astype(held_as)


def setup_inputs(seed: int = 0) -> dict:
    key_of = jax.random.split(jax.random.key(seed), 6)
    return {
        "layer_inputs": gaussian(key_of[0], (ROWS, LAYERS * D), 1.0, 6.0, ((0, 16), (1, 16))),
        "mlp_outputs": gaussian(key_of[1], (ROWS, LAYERS * D), 1.0, 6.0, ((0, 16), (1, 16))),
        "enc_weight": gaussian(key_of[2], (LAYERS * D, F), D ** -0.5, 0.125, ((0, 16), (1, 16))),
        "enc_bias": jnp.clip(-1.0 + 1.5 * jax.random.uniform(key_of[3], (LAYERS, F), jnp.float32) ** level_of(key_of[3], (LAYERS, F), ((1, 16),), -0.2, 0.2), -1.0, 0.5),
        "dec_weight": gaussian(key_of[4], (LAYERS, F, LAYERS * D), (LAYERS * F) ** -0.5, 0.03125, ((1, 16), (2, 16))),
    }


def reference(layer_inputs, mlp_outputs, enc_weight, enc_bias, dec_weight):
    rscale = ROWS ** -0.5
    pre_list = []
    latent_list = []
    for source in range(LAYERS):
        layer_in = layer_inputs[:, source * D:(source + 1) * D]
        pre_acts = jnp.dot(layer_in, enc_weight[source * D:(source + 1) * D], preferred_element_type=jnp.float32) + enc_bias[source][None, :]
        pre_list.append(pre_acts)
        latent_list.append(jnp.maximum(pre_acts, 0.0).astype(jnp.bfloat16))
    grad_list = []
    for target in range(LAYERS):
        recon = jnp.zeros((ROWS, D), jnp.float32)
        for source in range(target + 1):
            recon = recon + jnp.dot(latent_list[source], dec_weight[source, :, target * D:(target + 1) * D], preferred_element_type=jnp.float32)
        wanted = mlp_outputs[:, target * D:(target + 1) * D].astype(jnp.float32)
        grad_list.append(((recon - wanted) * rscale).astype(jnp.bfloat16))
    dec_rows = []
    enc_rows = []
    for source in range(LAYERS):
        blocks = []
        lat_grad = jnp.zeros((ROWS, F), jnp.float32)
        for target in range(LAYERS):
            if target >= source:
                piece = lax.dot_general(latent_list[source], grad_list[target], (((0,), (0,)), ((), ())), preferred_element_type=jnp.float32)
                blocks.append(piece.astype(jnp.bfloat16))
                weight = dec_weight[source, :, target * D:(target + 1) * D]
                lat_grad = lat_grad + lax.dot_general(grad_list[target], weight, (((1,), (1,)), ((), ())), preferred_element_type=jnp.float32)
            else:
                blocks.append(jnp.zeros((F, D), jnp.bfloat16))
        dec_rows.append(jnp.concatenate(blocks, axis=1))
        pre_grad = jnp.where(pre_list[source] > 0.0, lat_grad, 0.0).astype(jnp.bfloat16)
        layer_in = layer_inputs[:, source * D:(source + 1) * D]
        enc_rows.append(lax.dot_general(layer_in, pre_grad, (((0,), (0,)), ((), ())), preferred_element_type=jnp.float32))
    return jnp.concatenate(enc_rows, axis=0), jnp.stack(dec_rows, axis=0)
```

```python
import jax
import jax.numpy as jnp
from jax import lax
from jax.sharding import PartitionSpec as P


def from_partner(x, axis, bit):
    return lax.ppermute(x, axis, [(i, i ^ bit) for i in range(lax.axis_size(axis))])


def same_core_groups(size):
    return [[2 * k + core for k in range(size // 2)] for core in range(2)]


def exchanged(parts, axis, groups=None):
    return lax.all_to_all(
        parts, axis, split_axis=0, concat_axis=0, tiled=True, axis_index_groups=groups
    )


def rows_of_all(x):
    size = lax.axis_size("latent")
    chips = size // 2
    rows, width = x.shape
    copies = jnp.broadcast_to(x[None], (chips, rows, width))
    own = exchanged(copies, "latent", same_core_groups(size)).reshape(chips * rows, width)
    other = from_partner(own, "latent", 1)
    return jnp.concatenate([own, other], 0)


def rows_summed(x):
    size = lax.axis_size("latent")
    chips = size // 2
    half = x.shape[0] // 2
    theirs = from_partner(x[half:].astype(jnp.bfloat16), "latent", 1)
    both = (x[:half] + theirs.astype(jnp.float32)).astype(jnp.bfloat16)
    parts = both.reshape(chips, half // chips, x.shape[1])
    arrived = exchanged(parts, "latent", same_core_groups(size))
    return arrived.astype(jnp.float32).sum(axis=0)


def local(layer_inputs, mlp_outputs, enc_weight, enc_bias, dec_weight):
    position = lax.axis_index("layer")
    places = lax.axis_size("layer")
    layer_now = position // 2
    which_half = position % 2
    layer_count = places // 2
    latent_cols = enc_weight.shape[1]

    inputs_half = rows_of_all(layer_inputs)
    total_rows = inputs_half.shape[0]
    half_rows = total_rows // 2
    own_part = jnp.dot(inputs_half, enc_weight, preferred_element_type=jnp.float32)
    kept = lax.dynamic_slice_in_dim(own_part, which_half * half_rows, half_rows, 0)
    given = lax.dynamic_slice_in_dim(own_part, (1 - which_half) * half_rows, half_rows, 0)
    bias = lax.dynamic_slice_in_dim(enc_bias, layer_now, 1, 0)
    pre_half = kept + from_partner(given, "layer", 1) + bias
    latents_half = jnp.maximum(pre_half, 0.0).astype(jnp.bfloat16)

    copies = jnp.broadcast_to(latents_half[None], (places, half_rows, latent_cols))
    gathered = exchanged(copies, "layer").reshape(layer_count, total_rows, latent_cols)
    used = lax.broadcasted_iota(jnp.int32, (layer_count, 1, 1), 0) <= layer_now
    latents = jnp.where(used, gathered, jnp.zeros_like(gathered))

    recon = lax.dot_general(
        latents, dec_weight, (((0, 2), (0, 1)), ((), ())), preferred_element_type=jnp.float32
    )
    recon_own = rows_summed(recon)
    rscale = total_rows ** (-0.5)
    grad_own = ((recon_own - mlp_outputs.astype(jnp.float32)) * rscale).astype(jnp.bfloat16)
    out_grad = rows_of_all(grad_own)

    lat_terms = lax.dot_general(
        dec_weight, out_grad, (((2,), (1,)), ((), ())), preferred_element_type=jnp.float32
    )
    lat_terms = jnp.swapaxes(lat_terms, 1, 2).astype(jnp.bfloat16)
    dec_grad = lax.dot_general(
        latents, out_grad, (((1,), (0,)), ((), ())), preferred_element_type=jnp.float32
    ).astype(jnp.bfloat16)
    arrived = exchanged(lat_terms.reshape(places, half_rows, latent_cols), "layer")
    later = lax.broadcasted_iota(jnp.int32, (places, 1, 1), 0) // 2 >= layer_now
    lat_grad = jnp.where(later, arrived, jnp.zeros_like(arrived)).astype(jnp.float32).sum(axis=0)
    pre_grad = jnp.where(latents_half > 0, lat_grad, 0.0).astype(jnp.bfloat16)
    pre_other = from_partner(pre_grad, "layer", 1)
    first = which_half == 0
    pre_all = jnp.concatenate(
        [jnp.where(first, pre_grad, pre_other), jnp.where(first, pre_other, pre_grad)], 0
    )
    enc_grad = lax.dot_general(
        inputs_half, pre_all, (((0,), (0,)), ((), ())), preferred_element_type=jnp.float32
    )
    return (enc_grad, dec_grad)


def solution(mesh):
    in_specs = (
        P("latent", "layer"),
        P("latent", "layer"),
        P("layer", "latent"),
        P(None, "latent"),
        P(None, "latent", "layer"),
    )
    out_specs = (P("layer", "latent"), P(None, "latent", "layer"))
    return jax.shard_map(local, mesh=mesh, in_specs=in_specs, out_specs=out_specs, check_vma=False)
```

```python
import jax
import jax.numpy as jnp
from jax import lax
from jax.sharding import PartitionSpec as P


def from_partner(x, axis, bit):
    return lax.ppermute(x, axis, [(i, i ^ bit) for i in range(lax.axis_size(axis))])


def same_core_groups(size):
    return [[2 * k + core for k in range(size // 2)] for core in range(2)]


def exchanged(parts, axis, groups=None):
    return lax.all_to_all(
        parts, axis, split_axis=0, concat_axis=0, tiled=True, axis_index_groups=groups
    )


def along_ring(x):
    places, lanes = lax.axis_size("layer"), lax.axis_size("latent")
    ring = places // 2
    pairs = []
    for place in range(places):
        for lane in range(lanes):
            hop = 1 if lane % 2 == 0 else ring - 1
            target = (place // ring) * ring + (place % ring + hop) % ring
            pairs.append((place * lanes + lane, target * lanes + lane))
    return lax.ppermute(x, ("layer", "latent"), pairs)


def block_at(blocks, spot):
    return lax.dynamic_index_in_dim(blocks, spot % blocks.shape[1], 1, keepdims=False)


def added(a, b):
    return (a.astype(jnp.float32) + b.astype(jnp.float32)).astype(jnp.bfloat16)


def latents_of_all(own, plane, spot, way):
    places = lax.axis_size("layer")
    ring = places // 2
    lower = lax.ppermute(own, "layer", [(i, i + ring) for i in range(ring)])
    upper = plane == 1
    both = jnp.stack(
        [jnp.where(upper, lower, own), jnp.where(upper, own, jnp.zeros_like(own))], 0
    )
    stack = jnp.zeros((2, ring, *own.shape), own.dtype)

    def put(stack, block, where):
        return lax.dynamic_update_index_in_dim(stack, block, where % ring, 1)

    stack = put(stack, both, spot)
    moving = jnp.stack([both, from_partner(both, "latent", 1)], 0)
    for step in range(1, ring // 2):
        moving = along_ring(moving)
        stack = put(stack, moving[0], spot + ring - step * way)
        stack = put(stack, from_partner(moving[1], "latent", 1), spot + ring + step * way)
    return put(stack, along_ring(moving[0]), spot + ring // 2)


def terms_to_layers(terms, plane, spot, way):
    ring = terms.shape[1]
    far = ring // 2
    mine = [block_at(terms, spot + ring + step * way) for step in range(far + 1)]
    given = jnp.stack([block_at(terms, spot + ring - step * way) for step in range(1, far)], 0)
    taken = from_partner(given, "latent", 1)
    moving = along_ring(mine[far])
    moving = jnp.stack([added(mine[far - 1], moving), taken[far - 2]], 0)
    for step in range(far - 2, 0, -1):
        moving = added(along_ring(moving), jnp.stack([mine[step], taken[step - 1]], 0))
    moving = along_ring(moving)
    from_other = from_partner(moving[1], "latent", 1)
    total = (
        moving[0].astype(jnp.float32)
        + from_other.astype(jnp.float32)
        + mine[0].astype(jnp.float32)
    )
    crossed = lax.ppermute(
        total[0].astype(jnp.bfloat16), "layer", [(i + ring, i) for i in range(ring)]
    )
    return jnp.where(plane == 1, total[1], total[0] + crossed.astype(jnp.float32))


def rows_of_all(x):
    size = lax.axis_size("latent")
    chips = size // 2
    rows, width = x.shape
    copies = jnp.broadcast_to(x[None], (chips, rows, width))
    own = exchanged(copies, "latent", same_core_groups(size)).reshape(chips * rows, width)
    other = from_partner(own, "latent", 1)
    return jnp.concatenate([own, other], 0)


def rows_summed(x):
    size = lax.axis_size("latent")
    chips = size // 2
    half = x.shape[0] // 2
    theirs = from_partner(x[half:].astype(jnp.bfloat16), "latent", 1)
    both = (x[:half] + theirs.astype(jnp.float32)).astype(jnp.bfloat16)
    parts = both.reshape(chips, half // chips, x.shape[1])
    arrived = exchanged(parts, "latent", same_core_groups(size))
    return arrived.astype(jnp.float32).sum(axis=0)


def local(layer_inputs, mlp_outputs, enc_weight, enc_bias, dec_weight):
    position = lax.axis_index("layer")
    places = lax.axis_size("layer")
    layer_now = position // 2
    which_half = position % 2
    layer_count = places // 2
    latent_cols = enc_weight.shape[1]

    inputs_half = rows_of_all(layer_inputs)
    total_rows = inputs_half.shape[0]
    half_rows = total_rows // 2
    own_part = jnp.dot(inputs_half, enc_weight, preferred_element_type=jnp.float32)
    kept = lax.dynamic_slice_in_dim(own_part, which_half * half_rows, half_rows, 0)
    given = lax.dynamic_slice_in_dim(own_part, (1 - which_half) * half_rows, half_rows, 0)
    bias = lax.dynamic_slice_in_dim(enc_bias, layer_now, 1, 0)
    pre_half = kept + from_partner(given, "layer", 1) + bias
    latents_half = jnp.maximum(pre_half, 0.0).astype(jnp.bfloat16)

    ring = places // 2
    plane, spot = position // ring, position % ring
    way = 1 - 2 * (lax.axis_index("latent") % 2)
    gathered = latents_of_all(latents_half, plane, spot, way)
    gathered = gathered.reshape(layer_count, total_rows, latent_cols)
    used = lax.broadcasted_iota(jnp.int32, (layer_count, 1, 1), 0) <= layer_now
    latents = jnp.where(used, gathered, jnp.zeros_like(gathered))

    recon = lax.dot_general(
        latents, dec_weight, (((0, 2), (0, 1)), ((), ())), preferred_element_type=jnp.float32
    )
    recon_own = rows_summed(recon)
    rscale = total_rows ** (-0.5)
    grad_own = ((recon_own - mlp_outputs.astype(jnp.float32)) * rscale).astype(jnp.bfloat16)
    out_grad = rows_of_all(grad_own)

    lat_terms = lax.dot_general(
        dec_weight, out_grad, (((2,), (1,)), ((), ())), preferred_element_type=jnp.float32
    )
    lat_terms = jnp.where(used, jnp.swapaxes(lat_terms, 1, 2), 0.0).astype(jnp.bfloat16)
    dec_grad = lax.dot_general(
        latents, out_grad, (((1,), (0,)), ((), ())), preferred_element_type=jnp.float32
    ).astype(jnp.bfloat16)
    lat_grad = terms_to_layers(
        lat_terms.reshape(2, ring, half_rows, latent_cols), plane, spot, way
    )
    pre_grad = jnp.where(latents_half > 0, lat_grad, 0.0).astype(jnp.bfloat16)
    pre_other = from_partner(pre_grad, "layer", 1)
    first = which_half == 0
    pre_all = jnp.concatenate(
        [jnp.where(first, pre_grad, pre_other), jnp.where(first, pre_other, pre_grad)], 0
    )
    enc_grad = lax.dot_general(
        inputs_half, pre_all, (((0,), (0,)), ((), ())), preferred_element_type=jnp.float32
    )
    return (enc_grad, dec_grad)


def solution(mesh):
    in_specs = (
        P("latent", "layer"),
        P("latent", "layer"),
        P("layer", "latent"),
        P(None, "latent"),
        P(None, "latent", "layer"),
    )
    out_specs = (P("layer", "latent"), P(None, "latent", "layer"))
    return jax.shard_map(local, mesh=mesh, in_specs=in_specs, out_specs=out_specs, check_vma=False)
```

```python
import jax
import jax.numpy as jnp
from jax import lax
from jax.sharding import PartitionSpec as P


def from_partner(x, axis, bit):
    return lax.ppermute(x, axis, [(i, i ^ bit) for i in range(lax.axis_size(axis))])


def same_core_groups(size):
    return [[2 * k + core for k in range(size // 2)] for core in range(2)]


def exchanged(parts, axis, groups=None):
    return lax.all_to_all(
        parts, axis, split_axis=0, concat_axis=0, tiled=True, axis_index_groups=groups
    )


def along_ring(x, hop):
    places = lax.axis_size("layer")
    ring = places // 2
    pairs = [(i, (i // ring) * ring + (i % ring + hop) % ring) for i in range(places)]
    return lax.ppermute(x, "layer", pairs)


def to_later_plane(x):
    ring = lax.axis_size("layer") // 2
    return lax.ppermute(x, "layer", [(i, i + ring) for i in range(ring)])


def to_earlier_plane(x):
    ring = lax.axis_size("layer") // 2
    return lax.ppermute(x, "layer", [(i + ring, i) for i in range(ring)])


def added(*terms):
    return sum(term.astype(jnp.float32) for term in terms).astype(jnp.bfloat16)


def latents_of_all(own, plane, spot, ring):
    far = ring // 2
    half = own.shape[0] // 2
    stack = jnp.zeros((2 * ring, *own.shape), own.dtype)

    def put(stack, block, which, distance):
        place = which * ring + (spot + distance) % ring
        return lax.dynamic_update_index_in_dim(stack, block, place, 0)

    found = [(own, 0)]
    up = down = own
    bundles = []
    for step in range(1, far):
        up, down = along_ring(up, 1), along_ring(down, ring - 1)
        found += [(up, ring - step), (down, step)]
        if step == far // 2:
            crossed = to_later_plane(jnp.stack([block for block, _ in found], 0))
            bundles.append((crossed, [distance for _, distance in found]))
    ends = jnp.concatenate(
        [along_ring(up[:half], 1), along_ring(down[half:], ring - 1)], 0
    )
    found.append((ends, far))
    sent = len(bundles[0][1])
    crossed = to_later_plane(jnp.stack([block for block, _ in found[sent:]], 0))
    bundles.append((crossed, [distance for _, distance in found[sent:]]))
    for block, distance in found:
        stack = put(stack, block, plane, distance)
    for crossed, distances in bundles:
        for at, distance in enumerate(distances):
            stack = put(stack, crossed[at], 1 - plane, distance)
    return stack


def layer_terms(out_grad, weight, used):
    terms = lax.dot_general(
        weight, out_grad, (((2,), (1,)), ((), ())), preferred_element_type=jnp.float32
    )
    return jnp.where(used, jnp.swapaxes(terms, 1, 2), 0.0).astype(jnp.bfloat16)


def terms_to_layers(lower, own, spot, ring, tie):
    far = ring // 2
    half = own.shape[1] // 2

    def at(blocks, distance):
        return lax.dynamic_index_in_dim(blocks, (spot + distance) % ring, 0, keepdims=False)

    first = [far, far - 1, ring - far + 1]
    second = [d for d in range(ring) if d not in first]
    crossed = {}
    early = to_earlier_plane(jnp.stack([at(lower, d) for d in first], 0))
    late = to_earlier_plane(jnp.stack([at(lower, d) for d in second], 0))
    early, tie, own = lax.optimization_barrier((early, tie, own))
    for bundle, distances in ((early, first), (late, second)):
        for k, d in enumerate(distances):
            crossed[d] = bundle[k]
    ends = added(at(own, far), crossed[far])
    up, down = along_ring(ends[:half], 1), along_ring(ends[half:], ring - 1)
    for step in range(far - 1, 0, -1):
        back = ring - step
        if step == far - 1:
            up = jnp.concatenate([up, jnp.zeros_like(up)], 0)
            down = jnp.concatenate([jnp.zeros_like(down), down], 0)
        up = added(at(own, step), crossed[step], up)
        down = added(at(own, back), crossed[back], down)
        up, down = along_ring(up, 1), along_ring(down, ring - 1)
    total = sum(x.astype(jnp.float32) for x in (at(own, 0), crossed[0], up, down))
    return total, tie


def rows_of_all(x):
    size = lax.axis_size("latent")
    chips = size // 2
    rows, width = x.shape
    copies = jnp.broadcast_to(x[None], (chips, rows, width))
    own = exchanged(copies, "latent", same_core_groups(size)).reshape(chips * rows, width)
    other = from_partner(own, "latent", 1)
    return jnp.concatenate([own, other], 0)


def rows_summed(x):
    size = lax.axis_size("latent")
    chips = size // 2
    half = x.shape[0] // 2
    theirs = from_partner(x[half:].astype(jnp.bfloat16), "latent", 1)
    both = (x[:half] + theirs.astype(jnp.float32)).astype(jnp.bfloat16)
    parts = both.reshape(chips, half // chips, x.shape[1])
    arrived = exchanged(parts, "latent", same_core_groups(size))
    return arrived.astype(jnp.float32).sum(axis=0)


def local(layer_inputs, mlp_outputs, enc_weight, enc_bias, dec_weight):
    position = lax.axis_index("layer")
    places = lax.axis_size("layer")
    layer_now = position // 2
    which_half = position % 2
    layer_count = places // 2
    latent_cols = enc_weight.shape[1]

    inputs_half = rows_of_all(layer_inputs)
    total_rows = inputs_half.shape[0]
    half_rows = total_rows // 2
    own_part = jnp.dot(inputs_half, enc_weight, preferred_element_type=jnp.float32)
    kept = lax.dynamic_slice_in_dim(own_part, which_half * half_rows, half_rows, 0)
    given = lax.dynamic_slice_in_dim(own_part, (1 - which_half) * half_rows, half_rows, 0)
    bias = lax.dynamic_slice_in_dim(enc_bias, layer_now, 1, 0)
    pre_half = kept + from_partner(given, "layer", 1) + bias
    latents_half = jnp.maximum(pre_half, 0.0).astype(jnp.bfloat16)

    ring = places // 2
    plane, spot = position // ring, position % ring
    gathered = latents_of_all(latents_half, plane, spot, ring)
    gathered = gathered.reshape(layer_count, total_rows, latent_cols)
    used = lax.broadcasted_iota(jnp.int32, (layer_count, 1, 1), 0) <= layer_now
    latents = jnp.where(used, gathered, jnp.zeros_like(gathered))

    recon = lax.dot_general(
        latents, dec_weight, (((0, 2), (0, 1)), ((), ())), preferred_element_type=jnp.float32
    )
    recon_own = rows_summed(recon)
    rscale = total_rows ** (-0.5)
    grad_own = ((recon_own - mlp_outputs.astype(jnp.float32)) * rscale).astype(jnp.bfloat16)
    out_grad = rows_of_all(grad_own)

    near = layer_count // 2
    lower = layer_terms(out_grad, dec_weight[:near], used[:near])
    lower, grad_after = lax.optimization_barrier((lower, out_grad))
    upper = layer_terms(grad_after, dec_weight[near:], used[near:])
    own_terms = jnp.where(plane == 1, upper, lower)
    dec_grad = lax.dot_general(
        latents, grad_after, (((1,), (0,)), ((), ())), preferred_element_type=jnp.float32
    ).astype(jnp.bfloat16)
    places_shape = (ring, half_rows, latent_cols)
    lat_grad, dec_grad = terms_to_layers(
        lower.reshape(places_shape), own_terms.reshape(places_shape), spot, ring, dec_grad
    )
    pre_grad = jnp.where(latents_half > 0, lat_grad, 0.0).astype(jnp.bfloat16)
    pre_other = from_partner(pre_grad, "layer", 1)
    first = which_half == 0
    pre_all = jnp.concatenate(
        [jnp.where(first, pre_grad, pre_other), jnp.where(first, pre_other, pre_grad)], 0
    )
    enc_grad = lax.dot_general(
        inputs_half, pre_all, (((0,), (0,)), ((), ())), preferred_element_type=jnp.float32
    )
    return (enc_grad, dec_grad)


def solution(mesh):
    in_specs = (
        P("latent", "layer"),
        P("latent", "layer"),
        P("layer", "latent"),
        P(None, "latent"),
        P(None, "latent", "layer"),
    )
    out_specs = (P("layer", "latent"), P(None, "latent", "layer"))
    return jax.shard_map(local, mesh=mesh, in_specs=in_specs, out_specs=out_specs, check_vma=False)
```

```python
import jax
import jax.numpy as jnp
from jax import lax
from jax.sharding import PartitionSpec as P


def from_partner(x, axis, bit):
    return lax.ppermute(x, axis, [(i, i ^ bit) for i in range(lax.axis_size(axis))])


def same_core_groups(size):
    return [[2 * k + core for k in range(size // 2)] for core in range(2)]


def exchanged(parts, axis, groups=None):
    return lax.all_to_all(
        parts, axis, split_axis=0, concat_axis=0, tiled=True, axis_index_groups=groups
    )


def along_ring(x, hop):
    places = lax.axis_size("layer")
    ring = places // 2
    pairs = [(i, (i // ring) * ring + (i % ring + hop) % ring) for i in range(places)]
    return lax.ppermute(x, "layer", pairs)


def to_later_plane(x):
    ring = lax.axis_size("layer") // 2
    return lax.ppermute(x, "layer", [(i, i + ring) for i in range(ring)])


def to_earlier_plane(x):
    ring = lax.axis_size("layer") // 2
    return lax.ppermute(x, "layer", [(i + ring, i) for i in range(ring)])


def added(*terms):
    return sum(term.astype(jnp.float32) for term in terms).astype(jnp.bfloat16)


def latents_of_all(own, plane, spot, ring):
    half = own.shape[0] // 2
    stack = jnp.zeros((2 * ring, *own.shape), own.dtype)

    def put(stack, block, which, distance):
        place = which * ring + (spot + distance) % ring
        return lax.dynamic_update_index_in_dim(stack, block, place, 0)

    near = {0: own}
    for distance in (1, -1, 2, -2):
        near[distance] = along_ring(own, -distance)
    behind = along_ring(jnp.concatenate([near[-1], near[-2][:half]], 0), 2)
    ahead = along_ring(jnp.concatenate([near[1], near[2][half:]], 0), -2)
    near_order = list(near)
    near_crossed = to_later_plane(jnp.stack([near[d] for d in near_order], 0))
    far = {
        -3: behind[: 2 * half],
        3: ahead[: 2 * half],
        4: jnp.concatenate([behind[2 * half :], ahead[2 * half :]], 0),
    }
    far_order = list(far)
    far_crossed = to_later_plane(jnp.stack([far[d] for d in far_order], 0))
    for blocks, crossed, order in (
        (near, near_crossed, near_order),
        (far, far_crossed, far_order),
    ):
        for at, distance in enumerate(order):
            stack = put(stack, blocks[distance], plane, distance)
            stack = put(stack, crossed[at], 1 - plane, distance)
    return stack


def layer_terms(out_grad, weight, used):
    terms = lax.dot_general(
        weight, out_grad, (((2,), (1,)), ((), ())), preferred_element_type=jnp.float32
    )
    return jnp.where(used, jnp.swapaxes(terms, 1, 2), 0.0).astype(jnp.bfloat16)


def terms_to_layers(lower, own, spot, ring, tie):
    half = own.shape[1] // 2

    def at(blocks, distance):
        return lax.dynamic_index_in_dim(blocks, (spot + distance) % ring, 0, keepdims=False)

    first, second = (4, 3, -3), (1, -1, 2, -2, 0)
    early = to_earlier_plane(jnp.stack([at(lower, d) for d in first], 0))
    late = to_earlier_plane(jnp.stack([at(lower, d) for d in second], 0))
    early, tie, own = lax.optimization_barrier((early, tie, own))
    crossed = {d: early[k] for k, d in enumerate(first)}
    ends = added(at(own, 4), crossed[4])
    behind = along_ring(
        jnp.concatenate([added(at(own, 3), crossed[3]), ends[:half]], 0), 2
    )
    ahead = along_ring(
        jnp.concatenate([added(at(own, -3), crossed[-3]), ends[half:]], 0), -2
    )
    crossed = {d: late[k] for k, d in enumerate(second)}
    blank = jnp.zeros_like(ends[:half])
    arrived = [
        along_ring(added(at(own, 1), crossed[1], behind[: 2 * half]), 1),
        along_ring(added(at(own, -1), crossed[-1], ahead[: 2 * half]), -1),
        along_ring(
            added(at(own, 2), crossed[2], jnp.concatenate([behind[2 * half :], blank], 0)), 2
        ),
        along_ring(
            added(at(own, -2), crossed[-2], jnp.concatenate([blank, ahead[2 * half :]], 0)), -2
        ),
    ]
    total = sum(x.astype(jnp.float32) for x in (at(own, 0), crossed[0], *arrived))
    return total, tie


def rows_of_all(x):
    size = lax.axis_size("latent")
    chips = size // 2
    rows, width = x.shape
    copies = jnp.broadcast_to(x[None], (chips, rows, width))
    own = exchanged(copies, "latent", same_core_groups(size)).reshape(chips * rows, width)
    other = from_partner(own, "latent", 1)
    return jnp.concatenate([own, other], 0)


def rows_summed(x):
    size = lax.axis_size("latent")
    chips = size // 2
    half = x.shape[0] // 2
    theirs = from_partner(x[half:].astype(jnp.bfloat16), "latent", 1)
    both = (x[:half] + theirs.astype(jnp.float32)).astype(jnp.bfloat16)
    parts = both.reshape(chips, half // chips, x.shape[1])
    arrived = exchanged(parts, "latent", same_core_groups(size))
    return arrived.astype(jnp.float32).sum(axis=0)


def local(layer_inputs, mlp_outputs, enc_weight, enc_bias, dec_weight):
    position = lax.axis_index("layer")
    places = lax.axis_size("layer")
    layer_now = position // 2
    which_half = position % 2
    layer_count = places // 2
    latent_cols = enc_weight.shape[1]

    inputs_half = rows_of_all(layer_inputs)
    total_rows = inputs_half.shape[0]
    half_rows = total_rows // 2
    own_part = jnp.dot(inputs_half, enc_weight, preferred_element_type=jnp.float32)
    kept = lax.dynamic_slice_in_dim(own_part, which_half * half_rows, half_rows, 0)
    given = lax.dynamic_slice_in_dim(own_part, (1 - which_half) * half_rows, half_rows, 0)
    bias = lax.dynamic_slice_in_dim(enc_bias, layer_now, 1, 0)
    pre_half = kept + from_partner(given, "layer", 1) + bias
    latents_half = jnp.maximum(pre_half, 0.0).astype(jnp.bfloat16)

    ring = places // 2
    plane, spot = position // ring, position % ring
    gathered = latents_of_all(latents_half, plane, spot, ring)
    gathered = gathered.reshape(layer_count, total_rows, latent_cols)
    used = lax.broadcasted_iota(jnp.int32, (layer_count, 1, 1), 0) <= layer_now
    latents = jnp.where(used, gathered, jnp.zeros_like(gathered))

    recon = lax.dot_general(
        latents, dec_weight, (((0, 2), (0, 1)), ((), ())), preferred_element_type=jnp.float32
    )
    recon_own = rows_summed(recon)
    rscale = total_rows ** (-0.5)
    grad_own = ((recon_own - mlp_outputs.astype(jnp.float32)) * rscale).astype(jnp.bfloat16)
    out_grad = rows_of_all(grad_own)

    near = layer_count // 2
    lower = layer_terms(out_grad, dec_weight[:near], used[:near])
    lower, grad_after = lax.optimization_barrier((lower, out_grad))
    upper = layer_terms(grad_after, dec_weight[near:], used[near:])
    own_terms = jnp.where(plane == 1, upper, lower)
    dec_grad = lax.dot_general(
        latents, grad_after, (((1,), (0,)), ((), ())), preferred_element_type=jnp.float32
    ).astype(jnp.bfloat16)
    places_shape = (ring, half_rows, latent_cols)
    lat_grad, dec_grad = terms_to_layers(
        lower.reshape(places_shape), own_terms.reshape(places_shape), spot, ring, dec_grad
    )
    pre_grad = jnp.where(latents_half > 0, lat_grad, 0.0).astype(jnp.bfloat16)
    pre_other = from_partner(pre_grad, "layer", 1)
    first = which_half == 0
    pre_all = jnp.concatenate(
        [jnp.where(first, pre_grad, pre_other), jnp.where(first, pre_other, pre_grad)], 0
    )
    enc_grad = lax.dot_general(
        inputs_half, pre_all, (((0,), (0,)), ((), ())), preferred_element_type=jnp.float32
    )
    return (enc_grad, dec_grad)


def solution(mesh):
    in_specs = (
        P("latent", "layer"),
        P("latent", "layer"),
        P("layer", "latent"),
        P(None, "latent"),
        P(None, "latent", "layer"),
    )
    out_specs = (P("layer", "latent"), P(None, "latent", "layer"))
    return jax.shard_map(local, mesh=mesh, in_specs=in_specs, out_specs=out_specs, check_vma=False)
```

```python
import jax
import jax.numpy as jnp
from jax import lax
from jax.sharding import PartitionSpec as P


def from_partner(x, axis, bit):
    return lax.ppermute(x, axis, [(i, i ^ bit) for i in range(lax.axis_size(axis))])


def same_core_groups(size):
    return [[2 * k + core for k in range(size // 2)] for core in range(2)]


def exchanged(parts, axis, groups=None):
    return lax.all_to_all(
        parts, axis, split_axis=0, concat_axis=0, tiled=True, axis_index_groups=groups
    )


def along_ring(x, hop):
    places = lax.axis_size("layer")
    ring = places // 2
    pairs = [(i, (i // ring) * ring + (i % ring + hop) % ring) for i in range(places)]
    return lax.ppermute(x, "layer", pairs)


def to_later_plane(x):
    ring = lax.axis_size("layer") // 2
    return lax.ppermute(x, "layer", [(i, i + ring) for i in range(ring)])


def to_earlier_plane(x):
    ring = lax.axis_size("layer") // 2
    return lax.ppermute(x, "layer", [(i + ring, i) for i in range(ring)])


def added(*terms):
    return sum(term.astype(jnp.float32) for term in terms).astype(jnp.bfloat16)


def latents_of_all(own, plane, spot, ring):
    half = own.shape[0] // 2
    stack = jnp.zeros((2 * ring, *own.shape), own.dtype)

    def put(stack, block, which, distance):
        place = which * ring + (spot + distance) % ring
        at = (place % 2) * ring + place // 2
        return lax.dynamic_update_index_in_dim(stack, block, at, 0)

    near = {0: own, 1: along_ring(own, -1), -1: along_ring(own, 1)}
    bundles = [near]
    crossed = [to_later_plane(jnp.stack(list(near.values()), 0))]
    middle = {2: along_ring(own, -2), -2: along_ring(own, 2)}
    ready, middle = lax.optimization_barrier((near, middle))
    behind = along_ring(jnp.concatenate([ready[-1], middle[-2][:half]], 0), 2)
    ahead = along_ring(jnp.concatenate([ready[1], middle[2][half:]], 0), -2)
    bundles.append(middle)
    crossed.append(to_later_plane(jnp.stack(list(middle.values()), 0)))
    far = {
        -3: behind[: 2 * half],
        3: ahead[: 2 * half],
        4: jnp.concatenate([behind[2 * half :], ahead[2 * half :]], 0),
    }
    far, crossed[0] = lax.optimization_barrier((far, crossed[0]))
    bundles.append(far)
    crossed.append(to_later_plane(jnp.stack(list(far.values()), 0)))
    for blocks, others in zip(bundles, crossed):
        for at, distance in enumerate(blocks):
            stack = put(stack, blocks[distance], plane, distance)
            stack = put(stack, others[at], 1 - plane, distance)
    return stack


def layer_terms(out_grad, weight, used):
    terms = lax.dot_general(
        weight, out_grad, (((2,), (1,)), ((), ())), preferred_element_type=jnp.float32
    )
    return jnp.where(used, jnp.swapaxes(terms, 1, 2), 0.0).astype(jnp.bfloat16)


def terms_to_layers(lower, own, spot, ring, tie):
    rows = own[0].shape[1]
    half = rows // 2

    def at(blocks, distance):
        place = (spot + distance) % ring
        even, odd = [
            lax.dynamic_index_in_dim(part, place // 2, 0, keepdims=False) for part in blocks
        ]
        return jnp.where(place % 2 == 0, even, odd)

    first, second = (4, 3, -3), (1, -1, 2, -2, 0)
    early = to_earlier_plane(jnp.stack([at(lower, d) for d in first], 0))
    late = to_earlier_plane(jnp.stack([at(lower, d) for d in second], 0))
    early, tie, own = lax.optimization_barrier((early, tie, own))
    crossed = {d: early[k] for k, d in enumerate(first)}
    ends = added(at(own, 4), crossed[4])
    behind = along_ring(
        jnp.concatenate([added(at(own, 3), crossed[3]), ends[:half]], 0), 2
    )
    ahead = along_ring(
        jnp.concatenate([added(at(own, -3), crossed[-3]), ends[half:]], 0), -2
    )
    crossed = {d: late[k] for k, d in enumerate(second)}
    blank = jnp.zeros_like(ends[:half])
    arrived = [
        along_ring(added(at(own, 1), crossed[1], behind[: 2 * half]), 1),
        along_ring(added(at(own, -1), crossed[-1], ahead[: 2 * half]), -1),
        along_ring(
            added(at(own, 2), crossed[2], jnp.concatenate([behind[2 * half :], blank], 0)), 2
        ),
        along_ring(
            added(at(own, -2), crossed[-2], jnp.concatenate([blank, ahead[2 * half :]], 0)), -2
        ),
    ]
    total = sum(x.astype(jnp.float32) for x in (at(own, 0), crossed[0], *arrived))
    return total, tie


def own_core_rows(x):
    size = lax.axis_size("latent")
    chips = size // 2
    rows, width = x.shape
    copies = jnp.broadcast_to(x[None], (chips, rows, width))
    return exchanged(copies, "latent", same_core_groups(size)).reshape(chips * rows, width)


def rows_summed(own, other):
    size = lax.axis_size("latent")
    chips = size // 2
    theirs = from_partner(other.astype(jnp.bfloat16), "latent", 1)
    own, theirs = lax.optimization_barrier((own, theirs))
    both = (own + theirs.astype(jnp.float32)).astype(jnp.bfloat16)
    parts = both.reshape(chips, own.shape[0] // chips, own.shape[1])
    arrived = exchanged(parts, "latent", same_core_groups(size))
    return arrived.astype(jnp.float32).sum(axis=0)


def local(layer_inputs, mlp_outputs, enc_weight, enc_bias, dec_weight):
    position = lax.axis_index("layer")
    places = lax.axis_size("layer")
    layer_now = position // 2
    which_half = position % 2
    layer_count = places // 2
    latent_cols = enc_weight.shape[1]

    inputs_own = own_core_rows(layer_inputs)
    inputs_half = jnp.concatenate([inputs_own, from_partner(inputs_own, "latent", 1)], 0)
    total_rows = inputs_half.shape[0]
    half_rows = total_rows // 2
    own_part = jnp.dot(inputs_half, enc_weight, preferred_element_type=jnp.float32)
    kept = lax.dynamic_slice_in_dim(own_part, which_half * half_rows, half_rows, 0)
    given = lax.dynamic_slice_in_dim(own_part, (1 - which_half) * half_rows, half_rows, 0)
    bias = lax.dynamic_slice_in_dim(enc_bias, layer_now, 1, 0)
    pre_half = kept + from_partner(given, "layer", 1) + bias
    latents_half = jnp.maximum(pre_half, 0.0).astype(jnp.bfloat16)

    ring = places // 2
    plane, spot = position // ring, position % ring
    gathered = latents_of_all(latents_half, plane, spot, ring)
    gathered = gathered.reshape(2, layer_count, half_rows, latent_cols)
    used = lax.broadcasted_iota(jnp.int32, (layer_count, 1, 1), 0) <= layer_now
    latents = jnp.where(used, gathered, jnp.zeros_like(gathered))

    def decoded(part):
        return lax.dot_general(
            part, dec_weight, (((0, 2), (0, 1)), ((), ())), preferred_element_type=jnp.float32
        )

    recon_own = rows_summed(decoded(latents[0]), decoded(latents[1]))
    rscale = total_rows ** (-0.5)
    grad_own = ((recon_own - mlp_outputs.astype(jnp.float32)) * rscale).astype(jnp.bfloat16)
    grad_same = own_core_rows(grad_own)
    grad_other = from_partner(grad_same, "latent", 1)

    near = layer_count // 2
    lower_same = layer_terms(grad_same, dec_weight[:near], used[:near])
    lower_same, grad_other = lax.optimization_barrier((lower_same, grad_other))
    lower = (lower_same, layer_terms(grad_other, dec_weight[:near], used[:near]))
    lower, grads = lax.optimization_barrier((lower, (grad_same, grad_other)))
    upper = [layer_terms(grad, dec_weight[near:], used[near:]) for grad in grads]
    own_terms = [jnp.where(plane == 1, high, low) for high, low in zip(upper, lower)]
    dec_grad = lax.dot_general(
        latents,
        jnp.stack(grads, 0),
        (((0, 2), (0, 1)), ((), ())),
        preferred_element_type=jnp.float32,
    ).astype(jnp.bfloat16)
    lat_grad, dec_grad = terms_to_layers(lower, own_terms, spot, ring, dec_grad)
    pre_grad = jnp.where(latents_half > 0, lat_grad, 0.0).astype(jnp.bfloat16)
    pre_other = from_partner(pre_grad, "layer", 1)
    first = which_half == 0
    pre_all = jnp.concatenate(
        [jnp.where(first, pre_grad, pre_other), jnp.where(first, pre_other, pre_grad)], 0
    )
    enc_grad = lax.dot_general(
        inputs_half, pre_all, (((0,), (0,)), ((), ())), preferred_element_type=jnp.float32
    )
    return (enc_grad, dec_grad)


def solution(mesh):
    in_specs = (
        P("latent", "layer"),
        P("latent", "layer"),
        P("layer", "latent"),
        P(None, "latent"),
        P(None, "latent", "layer"),
    )
    out_specs = (P("layer", "latent"), P(None, "latent", "layer"))
    return jax.shard_map(local, mesh=mesh, in_specs=in_specs, out_specs=out_specs, check_vma=False)
```

```python
import jax
import jax.numpy as jnp
from jax import lax
from jax.sharding import PartitionSpec as P


def from_partner(x, axis, bit):
    return lax.ppermute(x, axis, [(i, i ^ bit) for i in range(lax.axis_size(axis))])


def same_core_groups(size):
    return [[2 * k + core for k in range(size // 2)] for core in range(2)]


def exchanged(parts, axis, groups=None):
    return lax.all_to_all(
        parts, axis, split_axis=0, concat_axis=0, tiled=True, axis_index_groups=groups
    )


def along_ring(x, hop):
    places = lax.axis_size("layer")
    ring = places // 2
    pairs = [(i, (i // ring) * ring + (i % ring + hop) % ring) for i in range(places)]
    return lax.ppermute(x, "layer", pairs)


def to_later_plane(x):
    ring = lax.axis_size("layer") // 2
    return lax.ppermute(x, "layer", [(i, i + ring) for i in range(ring)])


def to_earlier_plane(x):
    ring = lax.axis_size("layer") // 2
    return lax.ppermute(x, "layer", [(i + ring, i) for i in range(ring)])


def added(*terms):
    return sum(term.astype(jnp.float32) for term in terms).astype(jnp.bfloat16)


def latents_of_all(own, plane, spot, ring):
    half = own.shape[0] // 2
    stack = jnp.zeros((2 * ring, *own.shape), own.dtype)

    def put(stack, block, which, distance):
        place = which * ring + (spot + distance) % ring
        return lax.dynamic_update_index_in_dim(stack, block, place, 0)

    near = {0: own}
    for distance in (1, -1, 2, -2):
        near[distance] = along_ring(own, -distance)
    behind = along_ring(jnp.concatenate([near[-1], near[-2][:half]], 0), 2)
    ahead = along_ring(jnp.concatenate([near[1], near[2][half:]], 0), -2)
    near_order = list(near)
    near_crossed = to_later_plane(jnp.stack([near[d] for d in near_order], 0))
    far = {
        -3: behind[: 2 * half],
        3: ahead[: 2 * half],
        4: jnp.concatenate([behind[2 * half :], ahead[2 * half :]], 0),
    }
    far, near_crossed = lax.optimization_barrier((far, near_crossed))
    far_order = list(far)
    far_crossed = to_later_plane(jnp.stack([far[d] for d in far_order], 0))
    for blocks, crossed, order in (
        (near, near_crossed, near_order),
        (far, far_crossed, far_order),
    ):
        for at, distance in enumerate(order):
            stack = put(stack, blocks[distance], plane, distance)
            stack = put(stack, crossed[at], 1 - plane, distance)
    return stack


def layer_terms(out_grad, weight, used):
    terms = lax.dot_general(
        weight, out_grad, (((2,), (1,)), ((), ())), preferred_element_type=jnp.float32
    )
    return jnp.where(used, jnp.swapaxes(terms, 1, 2), 0.0).astype(jnp.bfloat16)


def terms_to_layers(lower, own, spot, ring, tie):
    half = own.shape[1] // 2

    def at(blocks, distance):
        return lax.dynamic_index_in_dim(blocks, (spot + distance) % ring, 0, keepdims=False)

    first, second = (4, 3, -3), (1, -1, 2, -2, 0)
    early = to_earlier_plane(jnp.stack([at(lower, d) for d in first], 0))
    late = to_earlier_plane(jnp.stack([at(lower, d) for d in second], 0))
    early, tie, own = lax.optimization_barrier((early, tie, own))
    crossed = {d: early[k] for k, d in enumerate(first)}
    ends = added(at(own, 4), crossed[4])
    behind = along_ring(
        jnp.concatenate([added(at(own, 3), crossed[3]), ends[:half]], 0), 2
    )
    ahead = along_ring(
        jnp.concatenate([added(at(own, -3), crossed[-3]), ends[half:]], 0), -2
    )
    crossed = {d: late[k] for k, d in enumerate(second)}
    blank = jnp.zeros_like(ends[:half])
    arrived = [
        along_ring(added(at(own, 1), crossed[1], behind[: 2 * half]), 1),
        along_ring(added(at(own, -1), crossed[-1], ahead[: 2 * half]), -1),
        along_ring(
            added(at(own, 2), crossed[2], jnp.concatenate([behind[2 * half :], blank], 0)), 2
        ),
        along_ring(
            added(at(own, -2), crossed[-2], jnp.concatenate([blank, ahead[2 * half :]], 0)), -2
        ),
    ]
    total = sum(x.astype(jnp.float32) for x in (at(own, 0), crossed[0], *arrived))
    return total, tie


def rows_of_all(x):
    size = lax.axis_size("latent")
    chips = size // 2
    rows, width = x.shape
    copies = jnp.broadcast_to(x[None], (chips, rows, width))
    own = exchanged(copies, "latent", same_core_groups(size)).reshape(chips * rows, width)
    other = from_partner(own, "latent", 1)
    return jnp.concatenate([own, other], 0)


def rows_summed(own, other):
    size = lax.axis_size("latent")
    chips = size // 2
    half = own.shape[0]
    theirs = from_partner(other.astype(jnp.bfloat16), "latent", 1)
    own, theirs = lax.optimization_barrier((own, theirs))
    both = (own + theirs.astype(jnp.float32)).astype(jnp.bfloat16)
    parts = both.reshape(chips, half // chips, own.shape[1])
    arrived = exchanged(parts, "latent", same_core_groups(size))
    return arrived.astype(jnp.float32).sum(axis=0)


def local(layer_inputs, mlp_outputs, enc_weight, enc_bias, dec_weight):
    position = lax.axis_index("layer")
    places = lax.axis_size("layer")
    layer_now = position // 2
    which_half = position % 2
    layer_count = places // 2
    latent_cols = enc_weight.shape[1]

    inputs_half = rows_of_all(layer_inputs)
    total_rows = inputs_half.shape[0]
    half_rows = total_rows // 2
    own_part = jnp.dot(inputs_half, enc_weight, preferred_element_type=jnp.float32)
    kept = lax.dynamic_slice_in_dim(own_part, which_half * half_rows, half_rows, 0)
    given = lax.dynamic_slice_in_dim(own_part, (1 - which_half) * half_rows, half_rows, 0)
    bias = lax.dynamic_slice_in_dim(enc_bias, layer_now, 1, 0)
    pre_half = kept + from_partner(given, "layer", 1) + bias
    latents_half = jnp.maximum(pre_half, 0.0).astype(jnp.bfloat16)

    ring = places // 2
    plane, spot = position // ring, position % ring
    gathered = latents_of_all(latents_half, plane, spot, ring)
    gathered = gathered.reshape(layer_count, total_rows, latent_cols)
    used = lax.broadcasted_iota(jnp.int32, (layer_count, 1, 1), 0) <= layer_now
    latents = jnp.where(used, gathered, jnp.zeros_like(gathered))

    def decoded(part):
        return lax.dot_general(
            part, dec_weight, (((0, 2), (0, 1)), ((), ())), preferred_element_type=jnp.float32
        )

    recon_own = rows_summed(
        decoded(latents[:, :half_rows]), decoded(latents[:, half_rows:])
    )
    rscale = total_rows ** (-0.5)
    grad_own = ((recon_own - mlp_outputs.astype(jnp.float32)) * rscale).astype(jnp.bfloat16)
    out_grad = rows_of_all(grad_own)

    near = layer_count // 2
    lower = layer_terms(out_grad, dec_weight[:near], used[:near])
    lower, grad_after = lax.optimization_barrier((lower, out_grad))
    upper = layer_terms(grad_after, dec_weight[near:], used[near:])
    own_terms = jnp.where(plane == 1, upper, lower)
    dec_grad = lax.dot_general(
        latents, grad_after, (((1,), (0,)), ((), ())), preferred_element_type=jnp.float32
    ).astype(jnp.bfloat16)
    places_shape = (ring, half_rows, latent_cols)
    lat_grad, dec_grad = terms_to_layers(
        lower.reshape(places_shape), own_terms.reshape(places_shape), spot, ring, dec_grad
    )
    pre_grad = jnp.where(latents_half > 0, lat_grad, 0.0).astype(jnp.bfloat16)
    pre_other = from_partner(pre_grad, "layer", 1)
    first = which_half == 0
    pre_all = jnp.concatenate(
        [jnp.where(first, pre_grad, pre_other), jnp.where(first, pre_other, pre_grad)], 0
    )
    enc_grad = lax.dot_general(
        inputs_half, pre_all, (((0,), (0,)), ((), ())), preferred_element_type=jnp.float32
    )
    return (enc_grad, dec_grad)


def solution(mesh):
    in_specs = (
        P("latent", "layer"),
        P("latent", "layer"),
        P("layer", "latent"),
        P(None, "latent"),
        P(None, "latent", "layer"),
    )
    out_specs = (P("layer", "latent"), P(None, "latent", "layer"))
    return jax.shard_map(local, mesh=mesh, in_specs=in_specs, out_specs=out_specs, check_vma=False)
```

```python
import jax
import jax.numpy as jnp
from jax import lax
from jax.sharding import PartitionSpec as P


def from_partner(x, axis, bit):
    return lax.ppermute(x, axis, [(i, i ^ bit) for i in range(lax.axis_size(axis))])


def same_core_groups(size):
    return [[2 * k + core for k in range(size // 2)] for core in range(2)]


def exchanged(parts, axis, groups=None):
    return lax.all_to_all(
        parts, axis, split_axis=0, concat_axis=0, tiled=True, axis_index_groups=groups
    )


def along_ring(x, hop):
    places = lax.axis_size("layer")
    ring = places // 2
    pairs = [(i, (i // ring) * ring + (i % ring + hop) % ring) for i in range(places)]
    return lax.ppermute(x, "layer", pairs)


def to_later_plane(x):
    ring = lax.axis_size("layer") // 2
    return lax.ppermute(x, "layer", [(i, i + ring) for i in range(ring)])


def to_earlier_plane(x):
    ring = lax.axis_size("layer") // 2
    return lax.ppermute(x, "layer", [(i + ring, i) for i in range(ring)])


def added(*terms):
    return sum(term.astype(jnp.float32) for term in terms).astype(jnp.bfloat16)


def latents_of_all(own, plane, spot, ring):
    half = own.shape[0] // 2
    stack = jnp.zeros((2 * ring, *own.shape), own.dtype)

    def put(stack, block, which, distance):
        place = which * ring + (spot + distance) % ring
        return lax.dynamic_update_index_in_dim(stack, block, place, 0)

    near = {0: own}
    for distance in (-2, 1, -1, 2):
        near[distance] = along_ring(own, -distance)
    behind = along_ring(jnp.concatenate([near[-1], near[-2][:half]], 0), 2)
    ahead = along_ring(jnp.concatenate([near[1], near[2][half:]], 0), -2)
    near_order = list(near)
    near_crossed = to_later_plane(jnp.stack([near[d] for d in near_order], 0))
    far = {
        -3: behind[: 2 * half],
        3: ahead[: 2 * half],
        4: jnp.concatenate([behind[2 * half :], ahead[2 * half :]], 0),
    }
    far, near_crossed = lax.optimization_barrier((far, near_crossed))
    far_order = list(far)
    far_crossed = to_later_plane(jnp.stack([far[d] for d in far_order], 0))
    for blocks, crossed, order in (
        (near, near_crossed, near_order),
        (far, far_crossed, far_order),
    ):
        for at, distance in enumerate(order):
            earlier = (spot + distance) % ring // 2 <= spot // 2
            block = jnp.where(earlier, blocks[distance], jnp.zeros_like(own))
            stack = put(stack, block, plane, distance)
            stack = put(stack, crossed[at], 1 - plane, distance)
    return stack


def layer_terms(out_grad, weight, used):
    terms = lax.dot_general(
        weight, out_grad, (((2,), (1,)), ((), ())), preferred_element_type=jnp.float32
    )
    return jnp.where(used, jnp.swapaxes(terms, 1, 2), 0.0).astype(jnp.bfloat16)


def terms_to_layers(lower, own, spot, ring, tie):
    half = own.shape[1] // 2

    def at(blocks, distance):
        return lax.dynamic_index_in_dim(blocks, (spot + distance) % ring, 0, keepdims=False)

    first, second = (4, 3, -3), (1, -1, 2, -2, 0)
    early = to_earlier_plane(jnp.stack([at(lower, d) for d in first], 0))
    late = to_earlier_plane(jnp.stack([at(lower, d) for d in second], 0))
    early, tie, own = lax.optimization_barrier((early, tie, own))
    crossed = {d: early[k] for k, d in enumerate(first)}
    ends = added(at(own, 4), crossed[4])
    behind = along_ring(
        jnp.concatenate([added(at(own, 3), crossed[3]), ends[:half]], 0), 2
    )
    ahead = along_ring(
        jnp.concatenate([added(at(own, -3), crossed[-3]), ends[half:]], 0), -2
    )
    crossed = {d: late[k] for k, d in enumerate(second)}
    blank = jnp.zeros_like(ends[:half])
    arrived = [
        along_ring(added(at(own, 1), crossed[1], behind[: 2 * half]), 1),
        along_ring(added(at(own, -1), crossed[-1], ahead[: 2 * half]), -1),
        along_ring(
            added(at(own, 2), crossed[2], jnp.concatenate([behind[2 * half :], blank], 0)), 2
        ),
        along_ring(
            added(at(own, -2), crossed[-2], jnp.concatenate([blank, ahead[2 * half :]], 0)), -2
        ),
    ]
    total = sum(x.astype(jnp.float32) for x in (at(own, 0), crossed[0], *arrived))
    return total, tie


def rows_of_all(x):
    size = lax.axis_size("latent")
    chips = size // 2
    rows, width = x.shape
    copies = jnp.broadcast_to(x[None], (chips, rows, width))
    own = exchanged(copies, "latent", same_core_groups(size)).reshape(chips * rows, width)
    other = from_partner(own, "latent", 1)
    return jnp.concatenate([own, other], 0)


def rows_summed(own, other):
    size = lax.axis_size("latent")
    chips = size // 2
    half = own.shape[0]
    theirs = from_partner(other.astype(jnp.bfloat16), "latent", 1)
    own, theirs = lax.optimization_barrier((own, theirs))
    both = (own + theirs.astype(jnp.float32)).astype(jnp.bfloat16)
    parts = both.reshape(chips, half // chips, own.shape[1])
    arrived = exchanged(parts, "latent", same_core_groups(size))
    return arrived.astype(jnp.float32).sum(axis=0)


def local(layer_inputs, mlp_outputs, enc_weight, enc_bias, dec_weight):
    position = lax.axis_index("layer")
    places = lax.axis_size("layer")
    layer_now = position // 2
    which_half = position % 2
    layer_count = places // 2
    latent_cols = enc_weight.shape[1]

    inputs_half = rows_of_all(layer_inputs)
    total_rows = inputs_half.shape[0]
    half_rows = total_rows // 2
    own_part = jnp.dot(inputs_half, enc_weight, preferred_element_type=jnp.float32)
    kept = lax.dynamic_slice_in_dim(own_part, which_half * half_rows, half_rows, 0)
    given = lax.dynamic_slice_in_dim(own_part, (1 - which_half) * half_rows, half_rows, 0)
    bias = lax.dynamic_slice_in_dim(enc_bias, layer_now, 1, 0)
    pre_half = kept + from_partner(given, "layer", 1) + bias
    latents_half = jnp.maximum(pre_half, 0.0).astype(jnp.bfloat16)

    ring = places // 2
    plane, spot = position // ring, position % ring
    gathered = latents_of_all(latents_half, plane, spot, ring)
    latents = gathered.reshape(layer_count, total_rows, latent_cols)
    used = lax.broadcasted_iota(jnp.int32, (layer_count, 1, 1), 0) <= layer_now

    def decoded(part):
        return lax.dot_general(
            part, dec_weight, (((0, 2), (0, 1)), ((), ())), preferred_element_type=jnp.float32
        )

    recon_own = rows_summed(
        decoded(latents[:, :half_rows]), decoded(latents[:, half_rows:])
    )
    rscale = total_rows ** (-0.5)
    grad_own = ((recon_own - mlp_outputs.astype(jnp.float32)) * rscale).astype(jnp.bfloat16)
    out_grad = rows_of_all(grad_own)

    near = layer_count // 2
    lower = layer_terms(out_grad, dec_weight[:near], used[:near])
    lower, grad_after = lax.optimization_barrier((lower, out_grad))
    upper = layer_terms(grad_after, dec_weight[near:], used[near:])
    own_terms = jnp.where(plane == 1, upper, lower)
    dec_grad = lax.dot_general(
        latents, grad_after, (((1,), (0,)), ((), ())), preferred_element_type=jnp.float32
    ).astype(jnp.bfloat16)
    places_shape = (ring, half_rows, latent_cols)
    lat_grad, dec_grad = terms_to_layers(
        lower.reshape(places_shape), own_terms.reshape(places_shape), spot, ring, dec_grad
    )
    pre_grad = jnp.where(latents_half > 0, lat_grad, 0.0).astype(jnp.bfloat16)
    pre_other = from_partner(pre_grad, "layer", 1)
    first = which_half == 0
    pre_all = jnp.concatenate(
        [jnp.where(first, pre_grad, pre_other), jnp.where(first, pre_other, pre_grad)], 0
    )
    enc_grad = lax.dot_general(
        inputs_half, pre_all, (((0,), (0,)), ((), ())), preferred_element_type=jnp.float32
    )
    return (enc_grad, dec_grad)


def solution(mesh):
    in_specs = (
        P("latent", "layer"),
        P("latent", "layer"),
        P("layer", "latent"),
        P(None, "latent"),
        P(None, "latent", "layer"),
    )
    out_specs = (P("layer", "latent"), P(None, "latent", "layer"))
    return jax.shard_map(local, mesh=mesh, in_specs=in_specs, out_specs=out_specs, check_vma=False)
```

```python
import jax
import jax.numpy as jnp
from jax import lax
from jax.sharding import PartitionSpec as P


def from_partner(x, axis, bit):
    return lax.ppermute(x, axis, [(i, i ^ bit) for i in range(lax.axis_size(axis))])


def same_core_groups(size):
    return [[2 * k + core for k in range(size // 2)] for core in range(2)]


def exchanged(parts, axis, groups=None):
    return lax.all_to_all(
        parts, axis, split_axis=0, concat_axis=0, tiled=True, axis_index_groups=groups
    )


def along_ring(x, hop):
    places = lax.axis_size("layer")
    ring = places // 2
    pairs = [(i, (i // ring) * ring + (i % ring + hop) % ring) for i in range(places)]
    return lax.ppermute(x, "layer", pairs)


def to_later_plane(x):
    ring = lax.axis_size("layer") // 2
    return lax.ppermute(x, "layer", [(i, i + ring) for i in range(ring)])


def to_earlier_plane(x):
    ring = lax.axis_size("layer") // 2
    return lax.ppermute(x, "layer", [(i + ring, i) for i in range(ring)])


def added(*terms):
    return sum(term.astype(jnp.float32) for term in terms).astype(jnp.bfloat16)


def latents_of_all(own, plane, spot, ring):
    half = own.shape[0] // 2
    stack = jnp.zeros((2 * ring, *own.shape), own.dtype)

    def put(stack, block, which, distance):
        place = which * ring + (spot + distance) % ring
        return lax.dynamic_update_index_in_dim(stack, block, place, 0)

    near = {0: own}
    for distance in (-2, 2, -1, 1):
        near[distance] = along_ring(own, -distance)
    behind = along_ring(jnp.concatenate([near[-1], near[-2][:half]], 0), 2)
    ahead = along_ring(jnp.concatenate([near[1], near[2][half:]], 0), -2)
    near_order = list(near)
    near_crossed = to_later_plane(jnp.stack([near[d] for d in near_order], 0))
    far = {
        -3: behind[: 2 * half],
        3: ahead[: 2 * half],
        4: jnp.concatenate([behind[2 * half :], ahead[2 * half :]], 0),
    }
    far, near_crossed = lax.optimization_barrier((far, near_crossed))
    far_order = list(far)
    far_crossed = to_later_plane(jnp.stack([far[d] for d in far_order], 0))
    for blocks, crossed, order in (
        (near, near_crossed, near_order),
        (far, far_crossed, far_order),
    ):
        for at, distance in enumerate(order):
            stack = put(stack, blocks[distance], plane, distance)
            stack = put(stack, crossed[at], 1 - plane, distance)
    return stack


def layer_terms(out_grad, weight, used):
    terms = lax.dot_general(
        weight, out_grad, (((2,), (1,)), ((), ())), preferred_element_type=jnp.float32
    )
    return jnp.where(used, jnp.swapaxes(terms, 1, 2), 0.0).astype(jnp.bfloat16)


def terms_to_layers(lower, own, spot, ring, tie):
    half = own.shape[1] // 2

    def at(blocks, distance):
        return lax.dynamic_index_in_dim(blocks, (spot + distance) % ring, 0, keepdims=False)

    first, second = (4, 3, -3), (1, -1, 2, -2, 0)
    early = to_earlier_plane(jnp.stack([at(lower, d) for d in first], 0))
    late = to_earlier_plane(jnp.stack([at(lower, d) for d in second], 0))
    early, tie, own = lax.optimization_barrier((early, tie, own))
    crossed = {d: early[k] for k, d in enumerate(first)}
    ends = added(at(own, 4), crossed[4])
    behind = along_ring(
        jnp.concatenate([added(at(own, 3), crossed[3]), ends[:half]], 0), 2
    )
    ahead = along_ring(
        jnp.concatenate([added(at(own, -3), crossed[-3]), ends[half:]], 0), -2
    )
    crossed = {d: late[k] for k, d in enumerate(second)}
    blank = jnp.zeros_like(ends[:half])
    arrived = [
        along_ring(added(at(own, 1), crossed[1], behind[: 2 * half]), 1),
        along_ring(added(at(own, -1), crossed[-1], ahead[: 2 * half]), -1),
        along_ring(
            added(at(own, 2), crossed[2], jnp.concatenate([behind[2 * half :], blank], 0)), 2
        ),
        along_ring(
            added(at(own, -2), crossed[-2], jnp.concatenate([blank, ahead[2 * half :]], 0)), -2
        ),
    ]
    total = sum(x.astype(jnp.float32) for x in (at(own, 0), crossed[0], *arrived))
    return total, tie


def rows_of_all(x):
    size = lax.axis_size("latent")
    chips = size // 2
    rows, width = x.shape
    copies = jnp.broadcast_to(x[None], (chips, rows, width))
    own = exchanged(copies, "latent", same_core_groups(size)).reshape(chips * rows, width)
    return own, from_partner(own, "latent", 1)


def rows_summed(own, other):
    size = lax.axis_size("latent")
    chips = size // 2
    half = own.shape[0]
    theirs = from_partner(other.astype(jnp.bfloat16), "latent", 1)
    own, theirs = lax.optimization_barrier((own, theirs))
    both = (own + theirs.astype(jnp.float32)).astype(jnp.bfloat16)
    parts = both.reshape(chips, half // chips, own.shape[1])
    arrived = exchanged(parts, "latent", same_core_groups(size))
    return arrived.astype(jnp.float32).sum(axis=0)


def local(layer_inputs, mlp_outputs, enc_weight, enc_bias, dec_weight):
    position = lax.axis_index("layer")
    places = lax.axis_size("layer")
    layer_now = position // 2
    which_half = position % 2
    layer_count = places // 2
    latent_cols = enc_weight.shape[1]

    inputs_pair = rows_of_all(layer_inputs)
    half_rows = inputs_pair[0].shape[0]
    total_rows = 2 * half_rows
    parts = [
        jnp.dot(rows, enc_weight, preferred_element_type=jnp.float32) for rows in inputs_pair
    ]
    first = which_half == 0
    kept = jnp.where(first, parts[0], parts[1])
    given = jnp.where(first, parts[1], parts[0])
    bias = lax.dynamic_slice_in_dim(enc_bias, layer_now, 1, 0)
    pre_half = kept + from_partner(given, "layer", 1) + bias
    latents_half = jnp.maximum(pre_half, 0.0).astype(jnp.bfloat16)

    ring = places // 2
    plane, spot = position // ring, position % ring
    gathered = latents_of_all(latents_half, plane, spot, ring)
    gathered = gathered.reshape(layer_count, total_rows, latent_cols)
    used = lax.broadcasted_iota(jnp.int32, (layer_count, 1, 1), 0) <= layer_now
    latents = jnp.where(used, gathered, jnp.zeros_like(gathered))

    def decoded(part):
        return lax.dot_general(
            part, dec_weight, (((0, 2), (0, 1)), ((), ())), preferred_element_type=jnp.float32
        )

    recon_own = rows_summed(
        decoded(latents[:, :half_rows]), decoded(latents[:, half_rows:])
    )
    rscale = total_rows ** (-0.5)
    grad_own = ((recon_own - mlp_outputs.astype(jnp.float32)) * rscale).astype(jnp.bfloat16)
    out_grad = jnp.concatenate(rows_of_all(grad_own), 0)

    near = layer_count // 2
    lower = layer_terms(out_grad, dec_weight[:near], used[:near])
    lower, grad_after = lax.optimization_barrier((lower, out_grad))
    upper = layer_terms(grad_after, dec_weight[near:], used[near:])
    own_terms = jnp.where(plane == 1, upper, lower)
    dec_grad = lax.dot_general(
        latents, grad_after, (((1,), (0,)), ((), ())), preferred_element_type=jnp.float32
    ).astype(jnp.bfloat16)
    places_shape = (ring, half_rows, latent_cols)
    lat_grad, dec_grad = terms_to_layers(
        lower.reshape(places_shape), own_terms.reshape(places_shape), spot, ring, dec_grad
    )
    pre_grad = jnp.where(latents_half > 0, lat_grad, 0.0).astype(jnp.bfloat16)
    pre_other = from_partner(pre_grad, "layer", 1)
    pre_all = jnp.concatenate(
        [jnp.where(first, pre_grad, pre_other), jnp.where(first, pre_other, pre_grad)], 0
    )
    enc_grad = lax.dot_general(
        jnp.concatenate(inputs_pair, 0), pre_all, (((0,), (0,)), ((), ())), preferred_element_type=jnp.float32
    )
    return (enc_grad, dec_grad)


def solution(mesh):
    in_specs = (
        P("latent", "layer"),
        P("latent", "layer"),
        P("layer", "latent"),
        P(None, "latent"),
        P(None, "latent", "layer"),
    )
    out_specs = (P("layer", "latent"), P(None, "latent", "layer"))
    return jax.shard_map(local, mesh=mesh, in_specs=in_specs, out_specs=out_specs, check_vma=False)
```

```python
import jax
import jax.numpy as jnp
from jax import lax
from jax.sharding import PartitionSpec as P


def from_partner(x, axis, bit):
    return lax.ppermute(x, axis, [(i, i ^ bit) for i in range(lax.axis_size(axis))])


def same_core_groups(size):
    return [[2 * k + core for k in range(size // 2)] for core in range(2)]


def exchanged(parts, axis, groups=None):
    return lax.all_to_all(
        parts, axis, split_axis=0, concat_axis=0, tiled=True, axis_index_groups=groups
    )


def along_ring(x, hop):
    places = lax.axis_size("layer")
    ring = places // 2
    pairs = [(i, (i // ring) * ring + (i % ring + hop) % ring) for i in range(places)]
    return lax.ppermute(x, "layer", pairs)


def to_later_plane(x):
    ring = lax.axis_size("layer") // 2
    return lax.ppermute(x, "layer", [(i, i + ring) for i in range(ring)])


def to_earlier_plane(x):
    ring = lax.axis_size("layer") // 2
    return lax.ppermute(x, "layer", [(i + ring, i) for i in range(ring)])


def added(*terms):
    return sum(term.astype(jnp.float32) for term in terms).astype(jnp.bfloat16)


def latents_of_all(own, plane, spot, ring):
    half = own.shape[0] // 2
    stack = jnp.zeros((2 * ring, *own.shape), own.dtype)

    def put(stack, block, which, distance):
        place = which * ring + (spot + distance) % ring
        return lax.dynamic_update_index_in_dim(stack, block, place, 0)

    near = {0: own}
    for distance in (-2, 2, -1, 1):
        near[distance] = along_ring(own, -distance)
    behind = along_ring(jnp.concatenate([near[-1], near[-2][:half]], 0), 2)
    ahead = along_ring(jnp.concatenate([near[1], near[2][half:]], 0), -2)
    near_order = list(near)
    near_crossed = to_later_plane(jnp.stack([near[d] for d in near_order], 0))
    far = {
        -3: behind[: 2 * half],
        3: ahead[: 2 * half],
        4: jnp.concatenate([behind[2 * half :], ahead[2 * half :]], 0),
    }
    far, near_crossed = lax.optimization_barrier((far, near_crossed))
    far_order = list(far)
    far_crossed = to_later_plane(jnp.stack([far[d] for d in far_order], 0))
    for blocks, crossed, order in (
        (near, near_crossed, near_order),
        (far, far_crossed, far_order),
    ):
        for at, distance in enumerate(order):
            stack = put(stack, blocks[distance], plane, distance)
            stack = put(stack, crossed[at], 1 - plane, distance)
    return stack


def layer_terms(out_grad, weight, used):
    terms = lax.dot_general(
        weight, out_grad, (((2,), (1,)), ((), ())), preferred_element_type=jnp.float32
    )
    return jnp.where(used, jnp.swapaxes(terms, 1, 2), 0.0).astype(jnp.bfloat16)


def terms_to_layers(lower, own, spot, ring, tie):
    half = own.shape[1] // 2

    def at(blocks, distance):
        return lax.dynamic_index_in_dim(blocks, (spot + distance) % ring, 0, keepdims=False)

    first, second = (4, 3, -3), (1, -1, 2, -2, 0)
    early = to_earlier_plane(jnp.stack([at(lower, d) for d in first], 0))
    late = to_earlier_plane(jnp.stack([at(lower, d) for d in second], 0))
    early, tie, own = lax.optimization_barrier((early, tie, own))
    crossed = {d: early[k] for k, d in enumerate(first)}
    ends = added(at(own, 4), crossed[4])
    behind = along_ring(
        jnp.concatenate([added(at(own, 3), crossed[3]), ends[:half]], 0), 2
    )
    ahead = along_ring(
        jnp.concatenate([added(at(own, -3), crossed[-3]), ends[half:]], 0), -2
    )
    crossed = {d: late[k] for k, d in enumerate(second)}
    blank = jnp.zeros_like(ends[:half])
    arrived = [
        along_ring(added(at(own, 1), crossed[1], behind[: 2 * half]), 1),
        along_ring(added(at(own, -1), crossed[-1], ahead[: 2 * half]), -1),
        along_ring(
            added(at(own, 2), crossed[2], jnp.concatenate([behind[2 * half :], blank], 0)), 2
        ),
        along_ring(
            added(at(own, -2), crossed[-2], jnp.concatenate([blank, ahead[2 * half :]], 0)), -2
        ),
    ]
    total = sum(x.astype(jnp.float32) for x in (at(own, 0), crossed[0], *arrived))
    return total, tie


def rows_of_all(x):
    size = lax.axis_size("latent")
    chips = size // 2
    rows, width = x.shape
    copies = jnp.broadcast_to(x[None], (chips, rows, width))
    own = exchanged(copies, "latent", same_core_groups(size)).reshape(chips * rows, width)
    return own, from_partner(own, "latent", 1)


def rows_summed(own, other):
    size = lax.axis_size("latent")
    chips = size // 2
    half = own.shape[0]
    theirs = from_partner(other.astype(jnp.bfloat16), "latent", 1)
    own, theirs = lax.optimization_barrier((own, theirs))
    both = (own + theirs.astype(jnp.float32)).astype(jnp.bfloat16)
    parts = both.reshape(chips, half // chips, own.shape[1])
    arrived = exchanged(parts, "latent", same_core_groups(size))
    return arrived.astype(jnp.float32).sum(axis=0)


def local(layer_inputs, mlp_outputs, enc_weight, enc_bias, dec_weight):
    position = lax.axis_index("layer")
    places = lax.axis_size("layer")
    layer_now = position // 2
    which_half = position % 2
    layer_count = places // 2
    latent_cols = enc_weight.shape[1]

    inputs_pair = rows_of_all(layer_inputs)
    half_rows = inputs_pair[0].shape[0]
    total_rows = 2 * half_rows
    parts = [
        jnp.dot(rows, enc_weight, preferred_element_type=jnp.float32) for rows in inputs_pair
    ]
    first = which_half == 0
    kept = jnp.where(first, parts[0], parts[1])
    given = jnp.where(first, parts[1], parts[0])
    bias = lax.dynamic_slice_in_dim(enc_bias, layer_now, 1, 0)
    pre_half = kept + from_partner(given, "layer", 1) + bias
    latents_half = jnp.maximum(pre_half, 0.0).astype(jnp.bfloat16)

    ring = places // 2
    plane, spot = position // ring, position % ring
    gathered = latents_of_all(latents_half, plane, spot, ring)
    gathered = gathered.reshape(layer_count, total_rows, latent_cols)
    used = lax.broadcasted_iota(jnp.int32, (layer_count, 1, 1), 0) <= layer_now
    latents = jnp.where(used, gathered, jnp.zeros_like(gathered))

    def decoded(part):
        return lax.dot_general(
            part, dec_weight, (((0, 2), (0, 1)), ((), ())), preferred_element_type=jnp.float32
        )

    recon_own = rows_summed(
        decoded(latents[:, :half_rows]), decoded(latents[:, half_rows:])
    )
    rscale = total_rows ** (-0.5)
    grad_own = ((recon_own - mlp_outputs.astype(jnp.float32)) * rscale).astype(jnp.bfloat16)
    grad_pair = rows_of_all(grad_own)
    out_grad = jnp.concatenate(grad_pair, 0)

    near = layer_count // 2
    lower = layer_terms(out_grad, dec_weight[:near], used[:near])
    lower, grad_pair = lax.optimization_barrier((lower, grad_pair))
    grad_after = jnp.concatenate(grad_pair, 0)
    upper = layer_terms(grad_after, dec_weight[near:], used[near:])
    own_terms = jnp.where(plane == 1, upper, lower)
    dec_grad = lax.dot_general(
        latents, grad_after, (((1,), (0,)), ((), ())), preferred_element_type=jnp.float32
    ).astype(jnp.bfloat16)
    places_shape = (ring, half_rows, latent_cols)
    lat_grad, dec_grad = terms_to_layers(
        lower.reshape(places_shape), own_terms.reshape(places_shape), spot, ring, dec_grad
    )
    pre_grad = jnp.where(latents_half > 0, lat_grad, 0.0).astype(jnp.bfloat16)
    pre_other = from_partner(pre_grad, "layer", 1)
    pre_all = jnp.concatenate(
        [jnp.where(first, pre_grad, pre_other), jnp.where(first, pre_other, pre_grad)], 0
    )
    enc_grad = lax.dot_general(
        jnp.concatenate(inputs_pair, 0), pre_all, (((0,), (0,)), ((), ())), preferred_element_type=jnp.float32
    )
    return (enc_grad, dec_grad)


def solution(mesh):
    in_specs = (
        P("latent", "layer"),
        P("latent", "layer"),
        P("layer", "latent"),
        P(None, "latent"),
        P(None, "latent", "layer"),
    )
    out_specs = (P("layer", "latent"), P(None, "latent", "layer"))
    return jax.shard_map(local, mesh=mesh, in_specs=in_specs, out_specs=out_specs, check_vma=False)
```
